32 devices in a mesh: grp: 16 (over z, x, core), seq: 1, prm: 2 (over y).
Axes of the slice: x: 2, y: 2, z: 4, core: 2. Of those that a mesh axis runs over, the one named last changes fastest.
Arguments:
- latent_before_step: bfloat16 [2, 16, 2, 64, 1536], P('prm', 'grp', None, 'seq'), may hold values from -40 to 40
- latent_after_step: bfloat16 [2, 16, 2, 64, 1536], P('prm', 'grp', None, 'seq'), may hold values from -6 to 6
- reference_step_means: bfloat16 [2, 16, 2, 64, 1536], P('prm', 'grp', None, 'seq'), may hold values from -6 to 6
- rewards: float32 [2, 16], P('prm', 'grp'), may hold values from -12 to 12
- sample_prompt_index: int32 [2, 16], P('prm', 'grp'), may hold values from 0 to 1, as said below
- stored_step_index: int32 [2, 16, 2], P('prm', 'grp'), may hold values from 1 to 9
- modulation: float32 [10, 2, 1536], replicated, may hold values from -3 to 3
- projection_weight: bfloat16 [1536, 2304], P(None, 'grp'), may hold values from -0.15625 to 0.15625
- output_weight: bfloat16 [768, 1536], P(None, 'grp'), may hold values from -0.21875 to 0.21875
- query_norm_gain: float32 [64], replicated, may hold values from 0.1 to 1.9
- key_norm_gain: float32 [64], replicated, may hold values from 0.1 to 1.9
- projection_down_weight: bfloat16 [1536, 32], replicated, may hold values from -0.15625 to 0.15625
- projection_up_weight: bfloat16 [32, 2304], replicated, may hold values from -1 to 1
- output_down_weight: bfloat16 [768, 32], replicated, may hold values from -0.21875 to 0.21875
- output_up_weight: bfloat16 [32, 1536], replicated, may hold values from -1 to 1
Outputs:
- grad_a_qkv: float32 [1536, 32], P('grp')
- projection_up_gradient: float32 [32, 2304], P(None, 'grp')
- grad_a_out: float32 [768, 32], P('grp')
- output_up_gradient: float32 [32, 1536], P(None, 'grp')
The draws below stay inside these ranges and needn't reach their ends.
Inputs may be any that keep to these rules, and one draw needn't show every extreme that they name: `sample_prompt_index`: in each row each of 0 and 1 stands exactly 8 times.
All inputs are finite; a program needn't handle non-finite values.
Results may differ from the reference program's by a relative error of at most 0.014.
Values may be sent and summed in bfloat16 or wider, within the bound.
A program may use at most 64 MiB of HBM per device.

```python
import math
import jax
import jax.numpy as jnp
from jax import lax

MODEL_DIMENSION = 1536
HEADS = 12
HDIM = 64
ADAPTER_RANK = 32
KSTEPS = 2
SCHED = 10
TOK_DEV = 64
TOKENS = 64
HEAD_FEATURES = 768
SAMPLES = 8
N_GRP = 16
N_SEQ = 1
N_PRM = 2


def draw_latent_before_step(key, part):
    noise_key, row_key, col_key = jax.random.split(key, 3)
    shape_full = (N_PRM, N_GRP, KSTEPS, TOKENS, MODEL_DIMENSION)
    half_span = 0.5 * math.log(10.0)
    row_scale = jnp.exp(jax.random.uniform(row_key, (N_PRM, N_GRP, KSTEPS, TOKENS, 1), jnp.float32, -half_span, half_span))
    col_scale = jnp.exp(jax.random.uniform(col_key, (N_PRM, N_GRP, KSTEPS, 1, MODEL_DIMENSION), jnp.float32, -half_span, half_span))
    base_values = jax.random.truncated_normal(noise_key, -4.0, 4.0, shape_full, jnp.float32)
    return (base_values * row_scale * col_scale).astype(jnp.bfloat16)


def draw_rewards(key, part):
    rising = 1.0 + 2.0 * jnp.arange(N_GRP, dtype=jnp.float32) / (N_GRP - 1)
    base_values = jax.random.truncated_normal(key, -4.0, 4.0, (N_PRM, N_GRP), jnp.float32)
    return base_values * rising[None, :]


def draw_sample_prompt_index(key, part):
    row_keys = jax.random.split(key, N_PRM)
    orders = jax.vmap(lambda row_key: jax.random.permutation(row_key, N_GRP))(row_keys)
    return (orders // (N_GRP // 2)).astype(jnp.int32)


def place_ends(result, rng, low, largest):
    extent = result.shape
    index_at = [jax.random.randint(jax.random.fold_in(rng, axis), (), 0, extent[axis]) for axis in range(len(extent))]
    result = result.at[tuple(index_at)].set(low)
    longest = extent.index(max(extent))
    index_at[longest] = (index_at[longest] + 1) % extent[longest]
    return result.at[tuple(index_at)].set(largest)


def shard_levels(key, extent, cuts, low, high):
    def one(dim, blocks):
        steps = jax.random.uniform(jax.random.fold_in(jax.random.fold_in(key, 6), dim), (blocks,), jnp.float32, low / len(cuts), high / len(cuts))
        return jnp.repeat(jnp.exp(steps), extent[dim] // blocks).reshape((-1,) + (1,) * (len(extent) - dim - 1))

    factor_of = one(*cuts[0])
    for cut in cuts[1:]:
        factor_of = factor_of * one(*cut)
    return factor_of


def bell_draw(stream_key, dims, width, reach, pieces=(), held_as=jnp.bfloat16):
    factor_of = shard_levels(stream_key, dims, pieces, -0.22, 0.18) if pieces else 1.0
    drawn = jax.random.normal(stream_key, dims, jnp.float32) * width * factor_of
    return jnp.minimum(jnp.maximum(drawn, -reach), reach).astype(held_as)


def setup_inputs(seed: int = 0) -> dict:
    keys = jax.random.split(jax.random.key(seed), 16)
    return {
        "latent_before_step": draw_latent_before_step(jax.random.fold_in(keys[15], 71), 0),
        "latent_after_step": bell_draw(keys[1], (N_PRM, N_GRP, KSTEPS, TOKENS, MODEL_DIMENSION), 1.0, 6.0, ((0, 2), (1, 16))),
        "reference_step_means": bell_draw(keys[2], (N_PRM, N_GRP, KSTEPS, TOKENS, MODEL_DIMENSION), 1.0, 6.0, ((0, 2), (1, 16))),
        "rewards": draw_rewards(jax.random.fold_in(keys[15], 71), 0),
        "sample_prompt_index": draw_sample_prompt_index(jax.random.fold_in(keys[15], 71), 0),
        "stored_step_index": place_ends(jax.random.randint(keys[5], (N_PRM, N_GRP, KSTEPS), 1, SCHED), jax.random.fold_in(keys[5], 1), 1, SCHED - 1).astype(jnp.int32),
        "modulation": bell_draw(keys[6], (SCHED, 2, MODEL_DIMENSION), 0.3, 3.0, (), jnp.float32),
        "projection_weight": bell_draw(keys[7], (MODEL_DIMENSION, 3 * HEAD_FEATURES), MODEL_DIMENSION ** -0.5, 0.15625, ((1, 16),)),
        "output_weight": bell_draw(keys[8], (HEAD_FEATURES, MODEL_DIMENSION), HEAD_FEATURES ** -0.5, 0.21875, ((1, 16),)),
        "query_norm_gain": jnp.clip(1.0 + 0.18 * jax.random.normal(keys[9], (HDIM,), jnp.float32), 0.1, 1.9),
        "key_norm_gain": jnp.clip(1.0 + 0.18 * jax.random.normal(keys[10], (HDIM,), jnp.float32), 0.1, 1.9),
        "projection_down_weight": bell_draw(keys[11], (MODEL_DIMENSION, ADAPTER_RANK), MODEL_DIMENSION ** -0.5, 0.15625),
        "projection_up_weight": bell_draw(keys[12], (ADAPTER_RANK, 3 * HEAD_FEATURES), ADAPTER_RANK ** -0.5, 1.0),
        "output_down_weight": bell_draw(keys[13], (HEAD_FEATURES, ADAPTER_RANK), HEAD_FEATURES ** -0.5, 0.21875),
        "output_up_weight": bell_draw(keys[14], (ADAPTER_RANK, MODEL_DIMENSION), ADAPTER_RANK ** -0.5, 1.0),
    }


ETA = 0.7
BETA = 0.1
ADAPTER_SCALE = 2.0

def rms_forward(values, gain_vec):
    inverse = lax.rsqrt(lax.optimization_barrier(jnp.mean(values * values, axis=-1, keepdims=True)) + 1e-06)
    return (values * inverse * gain_vec, inverse)

def rms_backward(values, inverse, gain_vec, upstream):
    scaled = upstream * gain_vec
    return inverse * scaled - values * inverse ** 3 * lax.optimization_barrier(jnp.mean(scaled * values, axis=-1, keepdims=True))

def per_sample_gradient(current_state_half, next_state_half, reference_half, timestep_values, advantage_values, sample_number, modulation, projection_weight, output_weight, query_norm_gain, key_norm_gain, projection_down_weight, projection_up_weight, output_down_weight, output_up_weight):
    row_count = KSTEPS * TOKENS
    score_scale = HDIM ** (-0.5)
    step_size = 1.0 / SCHED
    time_now = 1.0 - timestep_values.astype(jnp.float32) / SCHED
    variance = ETA * ETA * time_now / (1.0 - time_now) / SCHED
    coupling = ETA * ETA / (2.0 * (1.0 - time_now))
    mod_rows = modulation[timestep_values]
    shift_rows = mod_rows[:, 0][:, None, :]
    scale_rows = mod_rows[:, 1][:, None, :]
    state_now = current_state_half.astype(jnp.float32)
    centre = lax.optimization_barrier(jnp.mean(state_now, axis=-1, keepdims=True))
    spread = lax.optimization_barrier(jnp.mean((state_now - centre) ** 2, axis=-1, keepdims=True))
    normed = (state_now - centre) * lax.rsqrt(spread + 1e-06)
    input_rows = (normed * (1.0 + scale_rows) + shift_rows).astype(jnp.bfloat16).reshape(row_count, MODEL_DIMENSION)
    projection_lowrank = jnp.dot(input_rows, projection_down_weight, preferred_element_type=jnp.float32).astype(jnp.bfloat16)
    projected_rows = jnp.dot(input_rows, projection_weight, preferred_element_type=jnp.float32) + ADAPTER_SCALE * jnp.dot(projection_lowrank, projection_up_weight, preferred_element_type=jnp.float32)
    projected_rows = projected_rows.reshape(KSTEPS, TOKENS, 3, HEADS, HDIM)
    query_raw = projected_rows[:, :, 0]
    key_raw = projected_rows[:, :, 1]
    value_raw = projected_rows[:, :, 2]
    query_norm, query_inverse = rms_forward(query_raw, query_norm_gain)
    key_norm, key_inverse = rms_forward(key_raw, key_norm_gain)
    query_bf = query_norm.astype(jnp.bfloat16)
    key_bf = key_norm.astype(jnp.bfloat16)
    value_bf = value_raw.astype(jnp.bfloat16)
    scores = jnp.einsum('sqhd,skhd->shqk', query_bf.astype(jnp.float32), key_bf.astype(jnp.float32)) * score_scale
    weights = jnp.exp(scores)
    attn_probs = weights / lax.optimization_barrier(jnp.sum(weights, axis=-1, keepdims=True))
    probs_bf = attn_probs.astype(jnp.bfloat16)
    attended = jnp.einsum('shqk,skhd->sqhd', probs_bf.astype(jnp.float32), value_bf.astype(jnp.float32)).astype(jnp.bfloat16)
    attended_token_rows = attended.reshape(row_count, HEAD_FEATURES)
    output_lowrank = jnp.dot(attended_token_rows, output_down_weight, preferred_element_type=jnp.float32).astype(jnp.bfloat16)
    predicted_velocity = jnp.dot(attended_token_rows, output_weight, preferred_element_type=jnp.float32) + ADAPTER_SCALE * jnp.dot(output_lowrank, output_up_weight, preferred_element_type=jnp.float32)
    predicted_velocity = predicted_velocity.reshape(KSTEPS, TOKENS, MODEL_DIMENSION)
    time_col = time_now[:, None, None]
    var_col = variance[:, None, None]
    coup_col = coupling[:, None, None]
    mean_now = state_now - step_size * (predicted_velocity + coup_col * (state_now + (1.0 - time_col) * predicted_velocity))
    residual = next_state_half.astype(jnp.float32) - mean_now
    ref_drift = mean_now - reference_half.astype(jnp.float32)
    grad_mean = (-advantage_values * residual + BETA * ref_drift) / (sample_number * var_col)
    velocity_gradient = (grad_mean * (-step_size * (1.0 + coup_col * (1.0 - time_col)))).astype(jnp.bfloat16).reshape(row_count, MODEL_DIMENSION)
    output_up_gradient = ADAPTER_SCALE * jnp.dot(output_lowrank.T, velocity_gradient, preferred_element_type=jnp.float32)
    output_lowrank_gradient = (ADAPTER_SCALE * jnp.dot(velocity_gradient, output_up_weight.T, preferred_element_type=jnp.float32)).astype(jnp.bfloat16)
    grad_a_out = jnp.dot(attended_token_rows.T, output_lowrank_gradient, preferred_element_type=jnp.float32)
    attended_gradient = jnp.dot(velocity_gradient, output_weight.T, preferred_element_type=jnp.float32) + jnp.dot(output_lowrank_gradient, output_down_weight.T, preferred_element_type=jnp.float32)
    attended_gradient = attended_gradient.astype(jnp.bfloat16).reshape(KSTEPS, TOKENS, HEADS, HDIM)
    grad_probs = jnp.einsum('sqhd,skhd->shqk', attended_gradient.astype(jnp.float32), value_bf.astype(jnp.float32))
    row_delta = lax.optimization_barrier(jnp.sum(attended_gradient.astype(jnp.float32) * attended.astype(jnp.float32), axis=-1))
    row_delta = jnp.transpose(row_delta, (0, 2, 1))[..., None]
    grad_scores = (attn_probs * (grad_probs - row_delta) * score_scale).astype(jnp.bfloat16)
    grad_query = jnp.einsum('shqk,skhd->sqhd', grad_scores.astype(jnp.float32), key_bf.astype(jnp.float32))
    score_blocks = grad_scores.astype(jnp.float32).reshape(KSTEPS, HEADS, N_SEQ, TOK_DEV, TOKENS)
    prob_blocks = probs_bf.astype(jnp.float32).reshape(KSTEPS, HEADS, N_SEQ, TOK_DEV, TOKENS)
    query_blocks = query_bf.astype(jnp.float32).reshape(KSTEPS, N_SEQ, TOK_DEV, HEADS, HDIM)
    att_blocks = attended_gradient.astype(jnp.float32).reshape(KSTEPS, N_SEQ, TOK_DEV, HEADS, HDIM)
    key_part = jnp.einsum('shbqk,sbqhd->bskhd', score_blocks, query_blocks).astype(jnp.bfloat16)
    value_part = jnp.einsum('shbqk,sbqhd->bskhd', prob_blocks, att_blocks).astype(jnp.bfloat16)
    key_part = lax.optimization_barrier(key_part)
    value_part = lax.optimization_barrier(value_part)
    grad_key = lax.optimization_barrier(jnp.sum(key_part.astype(jnp.float32), axis=0))
    grad_value = lax.optimization_barrier(jnp.sum(value_part.astype(jnp.float32), axis=0))
    grad_q_raw = rms_backward(query_raw, query_inverse, query_norm_gain, grad_query)
    grad_k_raw = rms_backward(key_raw, key_inverse, key_norm_gain, grad_key)
    projected_gradient = jnp.stack([grad_q_raw, grad_k_raw, grad_value], axis=2).astype(jnp.bfloat16).reshape(row_count, 3 * HEAD_FEATURES)
    projection_up_gradient = ADAPTER_SCALE * jnp.dot(projection_lowrank.T, projected_gradient, preferred_element_type=jnp.float32)
    projection_lowrank_gradient = (ADAPTER_SCALE * jnp.dot(projected_gradient, projection_up_weight.T, preferred_element_type=jnp.float32)).astype(jnp.bfloat16)
    grad_a_qkv = jnp.dot(input_rows.T, projection_lowrank_gradient, preferred_element_type=jnp.float32)
    return (grad_a_qkv, projection_up_gradient, grad_a_out, output_up_gradient)

def flatten_samples(array_in):
    return array_in.reshape((N_PRM * N_GRP,) + array_in.shape[2:])

def reference(latent_before_step, latent_after_step, reference_step_means, rewards, sample_prompt_index, stored_step_index, modulation, projection_weight, output_weight, query_norm_gain, key_norm_gain, projection_down_weight, projection_up_weight, output_down_weight, output_up_weight):
    member = (sample_prompt_index[:, :, None] == jnp.arange(2, dtype=jnp.int32)[None, None, :]).astype(jnp.float32)
    totals = lax.optimization_barrier(jnp.sum(member * rewards[:, :, None], axis=1))
    baseline = lax.optimization_barrier(jnp.sum(member * totals[:, None, :], axis=-1)) / SAMPLES
    advantage_values = rewards - baseline
    sample_number = N_PRM * N_GRP * KSTEPS

    def accumulate(running, sample):
        current_state_half, next_state_half, reference_half, timestep_values, single_advantage = sample
        sample_pieces = per_sample_gradient(current_state_half, next_state_half, reference_half, timestep_values, single_advantage, sample_number, modulation, projection_weight, output_weight, query_norm_gain, key_norm_gain, projection_down_weight, projection_up_weight, output_down_weight, output_up_weight)
        return (tuple((total + extra for total, extra in zip(running, sample_pieces))), None)
    zero_grads = (jnp.zeros((MODEL_DIMENSION, ADAPTER_RANK), jnp.float32), jnp.zeros((ADAPTER_RANK, 3 * HEAD_FEATURES), jnp.float32), jnp.zeros((HEAD_FEATURES, ADAPTER_RANK), jnp.float32), jnp.zeros((ADAPTER_RANK, MODEL_DIMENSION), jnp.float32))
    summed, _ = lax.scan(accumulate, zero_grads, (flatten_samples(latent_before_step), flatten_samples(latent_after_step), flatten_samples(reference_step_means), flatten_samples(stored_step_index), advantage_values.reshape(-1)))
    return (summed[0], summed[1], summed[2], summed[3])
```

```python
import functools

import jax
import jax.numpy as jnp
from jax import lax
from jax.experimental import pallas as pl
from jax.experimental.pallas import tpu as pltpu
from jax.sharding import PartitionSpec as P

SCHED = 10


ETA = 0.7
BETA = 0.1
ADAPTER_SCALE = 2.0


def rms_forward(values, gain_vec):
    inverse = lax.rsqrt(jnp.mean(values * values, axis=-1, keepdims=True) + 1e-06)
    return (values * inverse * gain_vec, inverse)


def rms_backward(values, inverse, gain_vec, upstream):
    scaled = upstream * gain_vec
    return inverse * scaled - values * inverse**3 * jnp.mean(
        scaled * values, axis=-1, keepdims=True
    )


MESH = pl.DeviceIdType.MESH
CHIPS = 8
PART = 64


def ring_place(position):
    side = position // 4
    along = position * (1 - side) + (7 - position) * side
    return along * 2 + side


def enter(me, row, members):
    barrier = pltpu.get_barrier_semaphore()
    for offset in range(1, members):
        pl.semaphore_signal(
            barrier, inc=1, device_id=((me + offset) % members, 0, row), device_id_type=MESH
        )
    pl.semaphore_signal(barrier, inc=1, device_id=(me, 0, 1 - row), device_id_type=MESH)
    pl.semaphore_wait(barrier, members)


def gather_kernel(
    own_ref,
    note_ref,
    full_ref,
    notes_ref,
    ring_send,
    ring_recv,
    core_send,
    core_recv,
    row_send,
    row_recv,
    row_core_send,
    row_core_recv,
    own_sem,
    own_send,
    own_recv,
    note_send,
    note_recv,
    note_sem,
):
    me = lax.axis_index("grp")
    row = lax.axis_index("prm")
    core = me % 2
    side = (me // 2) % 2
    along = me // 4
    place = along * (1 - side) + (7 - along) * side
    sibling = (me - core + (1 - core), 0, row)
    partner = (me, 0, 1 - row)
    enter(me, row, 2 * CHIPS)

    def index_of(position):
        return ring_place((position + 2 * CHIPS) % CHIPS) * 2 + core

    def rows_of(part, of_row):
        start = 0 if part == 0 else pl.multiple_of(PART * (1 + of_row), PART)
        return pl.ds(start, PART)

    def remote(src, dst, send, recv, target):
        return pltpu.make_async_remote_copy(
            src_ref=src,
            dst_ref=dst,
            send_sem=send,
            recv_sem=recv,
            device_id=target,
            device_id_type=MESH,
        )

    def ring_copy(way, step, part):
        sign = 1 - 2 * way
        block = index_of(place - sign * step)
        rows = rows_of(part, row)
        src = own_ref.at[rows] if step == 0 else full_ref.at[block, rows]
        return remote(
            src,
            full_ref.at[block, rows],
            ring_send.at[way, step, part],
            ring_recv.at[way, step, part],
            (index_of(place + sign), 0, row),
        )

    def arrived(way, step):
        return index_of(place - (1 - 2 * way) * (step + 1))

    def valid(way, step, part):
        return step < 3 or (step == 3 and way == part)

    sends = []
    for part in range(2):
        for way in range(2):
            copy = ring_copy(way, 0, part)
            copy.start()
            sends.append(copy)
    notes = []
    for offset in range(1, 2 * CHIPS):
        copy = remote(
            note_ref,
            notes_ref.at[me],
            note_send.at[offset],
            note_recv.at[offset],
            ((me + offset) % (2 * CHIPS), 0, row),
        )
        copy.start()
        notes.append(copy)
    own_core = remote(own_ref, full_ref.at[me], own_send, own_recv, sibling)
    own_core.start()
    own_copy = pltpu.make_async_copy(own_ref, full_ref.at[me], own_sem)
    own_copy.start()
    note_copy = pltpu.make_async_copy(note_ref, notes_ref.at[me], note_sem)
    note_copy.start()

    relays = []
    rows_over = {}

    def row_arrivals(step):
        for way in range(2):
            if not valid(way, step, 1):
                continue
            rows_over[way, step].wait_recv()
            block = full_ref.at[arrived(way, step), rows_of(1, 1 - row)]
            copy = remote(
                block, block, row_core_send.at[way, step], row_core_recv.at[way, step], sibling
            )
            copy.start()
            relays.append(copy)

    for step in range(4):
        for part in range(2):
            for way in range(2):
                if not valid(way, step, part):
                    continue
                ring_copy(way, step, part).wait_recv()
                if valid(way, step + 1, part):
                    copy = ring_copy(way, step + 1, part)
                    copy.start()
                    sends.append(copy)
                block = full_ref.at[arrived(way, step), rows_of(part, row)]
                if part == 1:
                    copy = remote(
                        block, block, row_send.at[way, step], row_recv.at[way, step], partner
                    )
                    copy.start()
                    rows_over[way, step] = copy
                copy = remote(
                    block,
                    block,
                    core_send.at[way, step, part],
                    core_recv.at[way, step, part],
                    sibling,
                )
                copy.start()
                relays.append(copy)
        if step:
            row_arrivals(step - 1)
    row_arrivals(3)

    for copy in sends:
        copy.wait_send()
    for copy in rows_over.values():
        copy.wait_send()
    for copy in relays:
        copy.wait()
    for copy in notes:
        copy.wait()
    own_core.wait()
    own_copy.wait()
    note_copy.wait()


def gather_weights(own, note):
    members = 2 * CHIPS
    dma = pltpu.SemaphoreType.DMA
    return pl.pallas_call(
        gather_kernel,
        out_shape=(
            jax.ShapeDtypeStruct((members,) + own.shape, own.dtype),
            jax.ShapeDtypeStruct((members,) + note.shape, note.dtype),
        ),
        in_specs=[pl.BlockSpec(memory_space=pltpu.VMEM)] * 2,
        out_specs=(
            pl.BlockSpec(memory_space=pl.ANY),
            pl.BlockSpec(memory_space=pltpu.VMEM),
        ),
        scratch_shapes=[
            dma((2, 4, 2)),
            dma((2, 4, 2)),
            dma((2, 4, 2)),
            dma((2, 4, 2)),
            dma((2, 4)),
            dma((2, 4)),
            dma((2, 4)),
            dma((2, 4)),
            dma,
            dma,
            dma,
            dma((members,)),
            dma((members,)),
            dma,
        ],
        compiler_params=pltpu.CompilerParams(collective_id=0, has_side_effects=True),
        name="gather_weights",
    )(own, note)


def reduce_kernel(
    parts_ref, out_ref, landed, total, other, send_sem, recv_sem, row_send, row_recv
):
    me = lax.axis_index("grp")
    row = lax.axis_index("prm")
    members = parts_ref.shape[0]
    enter(me, row, members)
    copies = []
    for offset in range(1, members):
        target = (me + offset) % members
        copy = pltpu.make_async_remote_copy(
            src_ref=parts_ref.at[target],
            dst_ref=landed.at[offset],
            send_sem=send_sem.at[offset],
            recv_sem=recv_sem.at[offset],
            device_id=(target, 0, row),
            device_id_type=MESH,
        )
        copy.start()
        copies.append(copy)
    running = parts_ref[me].astype(jnp.float32)
    for offset in range(1, members):
        copies[offset - 1].wait_recv()
        running = running + landed[offset].astype(jnp.float32)
    total[...] = running
    swap = pltpu.make_async_remote_copy(
        src_ref=total,
        dst_ref=other,
        send_sem=row_send,
        recv_sem=row_recv,
        device_id=(me, 0, 1 - row),
        device_id_type=MESH,
    )
    swap.start()
    for copy in copies:
        copy.wait_send()
    swap.wait()
    out_ref[...] = total[...] + other[...]


def reduce_shares(parts):
    members = parts.shape[0]
    share = parts.shape[1:]
    dma = pltpu.SemaphoreType.DMA
    return pl.pallas_call(
        reduce_kernel,
        out_shape=jax.ShapeDtypeStruct(share, jnp.float32),
        in_specs=[pl.BlockSpec(memory_space=pltpu.VMEM)],
        out_specs=pl.BlockSpec(memory_space=pltpu.VMEM),
        scratch_shapes=[
            pltpu.VMEM(parts.shape, parts.dtype),
            pltpu.VMEM(share, jnp.float32),
            pltpu.VMEM(share, jnp.float32),
            dma((members,)),
            dma((members,)),
            dma,
            dma,
        ],
        compiler_params=pltpu.CompilerParams(collective_id=1, has_side_effects=True),
        name="reduce_shares",
    )(parts)


def direct_fits(projection_weight, output_weight):
    return (
        lax.axis_size("grp") == 2 * CHIPS
        and lax.axis_size("seq") == 1
        and lax.axis_size("prm") == 2
        and projection_weight.shape[1] + output_weight.shape[1] // 2 == 3 * PART
        and projection_weight.shape[0] == 2 * output_weight.shape[0]
    )


def per_device(
    latent_before_step,
    latent_after_step,
    reference_step_means,
    rewards,
    sample_prompt_index,
    stored_step_index,
    modulation,
    projection_weight,
    output_weight,
    query_norm_gain,
    key_norm_gain,
    projection_down_weight,
    projection_up_weight,
    output_down_weight,
    output_up_weight,
):
    steps_here = latent_before_step.shape[2]
    local_tokens = latent_before_step.shape[3]
    model_width = latent_before_step.shape[4]
    head_size = query_norm_gain.shape[0]
    inner_width = output_weight.shape[0]
    head_count = inner_width // head_size
    grp_count = lax.axis_size("grp")
    row_count = steps_here * local_tokens
    score_scale = head_size ** (-0.5)
    step_size = 1.0 / SCHED
    sample_number = lax.axis_size("prm") * grp_count * steps_here
    member = (sample_prompt_index[0, 0] == jnp.arange(2, dtype=jnp.int32)).astype(jnp.float32)
    reward = rewards[0, 0]
    direct = direct_fits(projection_weight, output_weight)
    if direct:
        half = output_weight.shape[1] // 2
        qkv_own = projection_weight.shape[1]
        own_out = output_weight.T
        own = jnp.concatenate(
            [projection_weight.T, jnp.concatenate([own_out[:half], own_out[half:]], axis=1)],
            axis=0,
        )
        note = jnp.broadcast_to(
            jnp.pad(member * reward, (0, 6))[:, None], (8, 128)
        )
        full, notes = gather_weights(own, note)
        totals = jnp.sum(notes[:, :2, 0], axis=0)
        full_qkv = full[:, :qkv_own].reshape(-1, model_width)
        full_out = (
            full[:, qkv_own:]
            .reshape(grp_count, half, 2, inner_width)
            .transpose(0, 2, 1, 3)
            .reshape(model_width, inner_width)
        )
    else:
        totals = lax.psum(member * reward, "grp")
        full_qkv, full_out = (
            lax.all_gather(projection_weight.T, "grp", axis=0, tiled=True),
            lax.all_gather(output_weight.T, "grp", axis=0, tiled=True),
        )
    advantage_values = reward - jnp.sum(member * totals) / (grp_count // 2)
    timestep_values = stored_step_index[0, 0]
    time_now = 1.0 - timestep_values.astype(jnp.float32) / SCHED
    variance = ETA * ETA * time_now / (1.0 - time_now) / SCHED
    coupling = ETA * ETA / (2.0 * (1.0 - time_now))
    mod_rows = jnp.take(modulation, timestep_values, axis=0)
    shift_rows = mod_rows[:, 0][:, None, :]
    scale_rows = mod_rows[:, 1][:, None, :]
    state_now = latent_before_step[0, 0].astype(jnp.float32)
    centre = jnp.mean(state_now, axis=-1, keepdims=True)
    spread = jnp.mean((state_now - centre) ** 2, axis=-1, keepdims=True)
    normed = (state_now - centre) * lax.rsqrt(spread + 1e-06)
    input_rows = (
        (normed * (1.0 + scale_rows) + shift_rows)
        .astype(jnp.bfloat16)
        .reshape(row_count, model_width)
    )
    projection_lowrank = jnp.dot(
        input_rows, projection_down_weight, preferred_element_type=jnp.float32
    ).astype(jnp.bfloat16)
    projected_rows = jnp.einsum(
        "rk,ck->rc", input_rows, full_qkv, preferred_element_type=jnp.float32
    ) + ADAPTER_SCALE * jnp.dot(
        projection_lowrank, projection_up_weight, preferred_element_type=jnp.float32
    )
    projected_rows = projected_rows.reshape(steps_here, local_tokens, 3, head_count, head_size)
    query_raw = projected_rows[:, :, 0]
    key_raw = projected_rows[:, :, 1]
    value_raw = projected_rows[:, :, 2]
    query_norm, query_inverse = rms_forward(query_raw, query_norm_gain)
    key_norm, key_inverse = rms_forward(key_raw, key_norm_gain)
    query_heads = jnp.transpose(query_norm.astype(jnp.bfloat16), (0, 2, 1, 3))
    key_local = jnp.transpose(key_norm.astype(jnp.bfloat16), (0, 2, 3, 1))
    value_local = jnp.transpose(value_raw.astype(jnp.bfloat16), (0, 2, 3, 1))
    key_cols, value_cols = (
        lax.all_gather(key_local, "seq", axis=3, tiled=True),
        lax.all_gather(value_local, "seq", axis=3, tiled=True),
    )
    scores = (
        jnp.einsum("shqd,shdk->shqk", query_heads, key_cols, preferred_element_type=jnp.float32)
        * score_scale
    )
    weights = jnp.exp(scores)
    attn_probs = weights / jnp.sum(weights, axis=-1, keepdims=True)
    probs_bf = attn_probs.astype(jnp.bfloat16)
    attended_heads = jnp.einsum(
        "shqk,shdk->shqd", probs_bf, value_cols, preferred_element_type=jnp.float32
    ).astype(jnp.bfloat16)
    attended_token_rows = jnp.transpose(attended_heads, (0, 2, 1, 3)).reshape(
        row_count, inner_width
    )
    output_lowrank = jnp.dot(
        attended_token_rows, output_down_weight, preferred_element_type=jnp.float32
    ).astype(jnp.bfloat16)
    predicted_velocity = jnp.einsum(
        "rk,ck->rc", attended_token_rows, full_out, preferred_element_type=jnp.float32
    ) + ADAPTER_SCALE * jnp.dot(
        output_lowrank, output_up_weight, preferred_element_type=jnp.float32
    )
    predicted_velocity = predicted_velocity.reshape(steps_here, local_tokens, model_width)
    time_col = time_now[:, None, None]
    var_col = variance[:, None, None]
    coup_col = coupling[:, None, None]
    mean_now = state_now - step_size * (
        predicted_velocity + coup_col * (state_now + (1.0 - time_col) * predicted_velocity)
    )
    residual = latent_after_step[0, 0].astype(jnp.float32) - mean_now
    ref_drift = mean_now - reference_step_means[0, 0].astype(jnp.float32)
    grad_mean = (-advantage_values * residual + BETA * ref_drift) / (sample_number * var_col)
    velocity_gradient = (
        (grad_mean * (-step_size * (1.0 + coup_col * (1.0 - time_col))))
        .astype(jnp.bfloat16)
        .reshape(row_count, model_width)
    )
    output_up_gradient = ADAPTER_SCALE * jnp.dot(
        output_lowrank.T, velocity_gradient, preferred_element_type=jnp.float32
    )
    output_lowrank_gradient = (
        ADAPTER_SCALE
        * jnp.dot(velocity_gradient, output_up_weight.T, preferred_element_type=jnp.float32)
    ).astype(jnp.bfloat16)
    grad_a_out = jnp.dot(
        attended_token_rows.T, output_lowrank_gradient, preferred_element_type=jnp.float32
    )
    attended_gradient = jnp.dot(
        velocity_gradient, full_out, preferred_element_type=jnp.float32
    ) + jnp.dot(output_lowrank_gradient, output_down_weight.T, preferred_element_type=jnp.float32)
    grad_att_heads = jnp.transpose(
        attended_gradient.astype(jnp.bfloat16).reshape(
            steps_here, local_tokens, head_count, head_size
        ),
        (0, 2, 1, 3),
    )
    grad_probs = jnp.einsum(
        "shqd,shdk->shqk", grad_att_heads, value_cols, preferred_element_type=jnp.float32
    )
    row_delta = jnp.sum(
        grad_att_heads.astype(jnp.float32) * attended_heads.astype(jnp.float32),
        axis=-1,
        keepdims=True,
    )
    grad_scores = (attn_probs * (grad_probs - row_delta) * score_scale).astype(jnp.bfloat16)
    grad_query_heads = jnp.einsum(
        "shqk,shdk->shqd", grad_scores, key_cols, preferred_element_type=jnp.float32
    )
    grad_query = jnp.transpose(grad_query_heads, (0, 2, 1, 3))
    key_term = jnp.einsum(
        "shqk,shqd->shdk", grad_scores, query_heads, preferred_element_type=jnp.float32
    )
    value_term = jnp.einsum(
        "shqk,shqd->shdk", probs_bf, grad_att_heads, preferred_element_type=jnp.float32
    )
    key_owned, value_owned = (
        lax.psum_scatter(
            key_term.astype(jnp.bfloat16), "seq", scatter_dimension=3, tiled=True
        ).astype(jnp.float32),
        lax.psum_scatter(
            value_term.astype(jnp.bfloat16), "seq", scatter_dimension=3, tiled=True
        ).astype(jnp.float32),
    )
    grad_key = jnp.transpose(key_owned, (0, 3, 1, 2))
    grad_value = jnp.transpose(value_owned, (0, 3, 1, 2))
    grad_q_raw = rms_backward(query_raw, query_inverse, query_norm_gain, grad_query)
    grad_k_raw = rms_backward(key_raw, key_inverse, key_norm_gain, grad_key)
    projected_gradient = (
        jnp.stack([grad_q_raw, grad_k_raw, grad_value], axis=2)
        .astype(jnp.bfloat16)
        .reshape(row_count, 3 * inner_width)
    )
    projection_up_gradient = ADAPTER_SCALE * jnp.dot(
        projection_lowrank.T, projected_gradient, preferred_element_type=jnp.float32
    )
    projection_lowrank_gradient = (
        ADAPTER_SCALE
        * jnp.dot(projected_gradient, projection_up_weight.T, preferred_element_type=jnp.float32)
    ).astype(jnp.bfloat16)
    grad_a_qkv = jnp.dot(
        input_rows.T, projection_lowrank_gradient, preferred_element_type=jnp.float32
    )
    local_grads = (grad_a_qkv, projection_up_gradient, grad_a_out, output_up_gradient)
    rank = projection_lowrank.shape[1]
    wide = (local_grads[0].T, local_grads[1], local_grads[2].T, local_grads[3])
    widths = [grad.shape[1] // grp_count for grad in wide]
    packed = jnp.concatenate(
        [
            grad.astype(jnp.bfloat16).reshape(rank, grp_count, width)
            for grad, width in zip(wide, widths)
        ],
        axis=2,
    )
    if direct:
        share = reduce_shares(packed.transpose(1, 0, 2))
    else:
        share = lax.psum_scatter(
            packed, "grp", scatter_dimension=1, tiled=True
        ).astype(jnp.float32).reshape(rank, -1)
        share = lax.psum(share, ("seq", "prm"))
    first, second, third = widths[0], widths[0] + widths[1], sum(widths[:3])
    return (
        share[:, :first].T,
        share[:, first:second],
        share[:, second:third].T,
        share[:, third:],
    )


def solution(mesh):
    in_specs = (
        P("prm", "grp", None, "seq", None),
        P("prm", "grp", None, "seq", None),
        P("prm", "grp", None, "seq", None),
        P("prm", "grp"),
        P("prm", "grp"),
        P("prm", "grp", None),
        P(),
        P(None, "grp"),
        P(None, "grp"),
        P(),
        P(),
        P(),
        P(),
        P(),
        P(),
    )
    out_specs = (P("grp", None), P(None, "grp"), P("grp", None), P(None, "grp"))
    return jax.shard_map(
        per_device, mesh=mesh, in_specs=in_specs, out_specs=out_specs, check_vma=False
    )
```

```python
import functools

import jax
import jax.numpy as jnp
from jax import lax
from jax.experimental import pallas as pl
from jax.experimental.pallas import tpu as pltpu
from jax.sharding import PartitionSpec as P

SCHED = 10


ETA = 0.7
BETA = 0.1
ADAPTER_SCALE = 2.0


def rms_forward(values, gain_vec):
    inverse = lax.rsqrt(jnp.mean(values * values, axis=-1, keepdims=True) + 1e-06)
    return (values * inverse * gain_vec, inverse)


def rms_backward(values, inverse, gain_vec, upstream):
    scaled = upstream * gain_vec
    return inverse * scaled - values * inverse**3 * jnp.mean(
        scaled * values, axis=-1, keepdims=True
    )


MESH = pl.DeviceIdType.MESH
CHIPS = 8
PART = 64


def ring_place(position):
    side = position // 4
    along = position * (1 - side) + (7 - position) * side
    return along * 2 + side


def enter(me, row, members):
    barrier = pltpu.get_barrier_semaphore()
    for offset in range(1, members):
        pl.semaphore_signal(
            barrier, inc=1, device_id=((me + offset) % members, 0, row), device_id_type=MESH
        )
    pl.semaphore_signal(barrier, inc=1, device_id=(me, 0, 1 - row), device_id_type=MESH)
    pl.semaphore_wait(barrier, members)


def gather_kernel(
    own_ref,
    note_ref,
    full_ref,
    notes_ref,
    ring_send,
    ring_recv,
    core_send,
    core_recv,
    row_send,
    row_recv,
    row_core_send,
    row_core_recv,
    own_sem,
    own_send,
    own_recv,
    note_send,
    note_recv,
    note_sem,
):
    me = lax.axis_index("grp")
    row = lax.axis_index("prm")
    core = me % 2
    side = (me // 2) % 2
    along = me // 4
    place = along * (1 - side) + (7 - along) * side
    sibling = (me - core + (1 - core), 0, row)
    partner = (me, 0, 1 - row)
    enter(me, row, 2 * CHIPS)

    def index_of(position):
        return ring_place((position + 2 * CHIPS) % CHIPS) * 2 + core

    def rows_of(part, of_row):
        start = 0 if part == 0 else pl.multiple_of(PART * (1 + of_row), PART)
        return pl.ds(start, PART)

    def remote(src, dst, send, recv, target):
        return pltpu.make_async_remote_copy(
            src_ref=src,
            dst_ref=dst,
            send_sem=send,
            recv_sem=recv,
            device_id=target,
            device_id_type=MESH,
        )

    def ring_copy(way, step, part):
        sign = 1 - 2 * way
        block = index_of(place - sign * step)
        rows = rows_of(part, row)
        src = own_ref.at[rows] if step == 0 else full_ref.at[block, rows]
        return remote(
            src,
            full_ref.at[block, rows],
            ring_send.at[way, step, part],
            ring_recv.at[way, step, part],
            (index_of(place + sign), 0, row),
        )

    def arrived(way, step):
        return index_of(place - (1 - 2 * way) * (step + 1))

    def valid(way, step, part):
        return step < 3 or (step == 3 and way == part)

    sends = []
    for part in range(2):
        for way in range(2):
            copy = ring_copy(way, 0, part)
            copy.start()
            sends.append(copy)
    notes = []
    for offset in range(1, 2 * CHIPS):
        copy = remote(
            note_ref,
            notes_ref.at[me],
            note_send.at[offset],
            note_recv.at[offset],
            ((me + offset) % (2 * CHIPS), 0, row),
        )
        copy.start()
        notes.append(copy)
    own_core = remote(own_ref, full_ref.at[me], own_send, own_recv, sibling)
    own_core.start()
    own_copy = pltpu.make_async_copy(own_ref, full_ref.at[me], own_sem)
    own_copy.start()
    note_copy = pltpu.make_async_copy(note_ref, notes_ref.at[me], note_sem)
    note_copy.start()

    relays = []
    rows_over = {}

    def row_arrivals(step):
        for way in range(2):
            if not valid(way, step, 1):
                continue
            rows_over[way, step].wait_recv()
            block = full_ref.at[arrived(way, step), rows_of(1, 1 - row)]
            copy = remote(
                block, block, row_core_send.at[way, step], row_core_recv.at[way, step], sibling
            )
            copy.start()
            relays.append(copy)

    for step in range(4):
        for part in range(2):
            for way in range(2):
                if not valid(way, step, part):
                    continue
                ring_copy(way, step, part).wait_recv()
                if valid(way, step + 1, part):
                    copy = ring_copy(way, step + 1, part)
                    copy.start()
                    sends.append(copy)
                block = full_ref.at[arrived(way, step), rows_of(part, row)]
                if part == 1:
                    copy = remote(
                        block, block, row_send.at[way, step], row_recv.at[way, step], partner
                    )
                    copy.start()
                    rows_over[way, step] = copy
                copy = remote(
                    block,
                    block,
                    core_send.at[way, step, part],
                    core_recv.at[way, step, part],
                    sibling,
                )
                copy.start()
                relays.append(copy)
        if step:
            row_arrivals(step - 1)
    row_arrivals(3)

    for copy in sends:
        copy.wait_send()
    for copy in rows_over.values():
        copy.wait_send()
    for copy in relays:
        copy.wait()
    for copy in notes:
        copy.wait()
    own_core.wait()
    own_copy.wait()
    note_copy.wait()


def gather_weights(own, note):
    members = 2 * CHIPS
    dma = pltpu.SemaphoreType.DMA
    return pl.pallas_call(
        gather_kernel,
        out_shape=(
            jax.ShapeDtypeStruct((members,) + own.shape, own.dtype),
            jax.ShapeDtypeStruct((members,) + note.shape, note.dtype),
        ),
        in_specs=[pl.BlockSpec(memory_space=pltpu.VMEM)] * 2,
        out_specs=(
            pl.BlockSpec(memory_space=pl.ANY),
            pl.BlockSpec(memory_space=pltpu.VMEM),
        ),
        scratch_shapes=[
            dma((2, 4, 2)),
            dma((2, 4, 2)),
            dma((2, 4, 2)),
            dma((2, 4, 2)),
            dma((2, 4)),
            dma((2, 4)),
            dma((2, 4)),
            dma((2, 4)),
            dma,
            dma,
            dma,
            dma((members,)),
            dma((members,)),
            dma,
        ],
        compiler_params=pltpu.CompilerParams(collective_id=0, has_side_effects=True),
        name="gather_weights",
    )(own, note)


def reduce_kernel(
    parts_ref, out_ref, landed, total, other, send_sem, recv_sem, row_send, row_recv
):
    me = lax.axis_index("grp")
    row = lax.axis_index("prm")
    members = parts_ref.shape[0]
    enter(me, row, members)
    copies = []
    for offset in range(1, members):
        target = (me + offset) % members
        copy = pltpu.make_async_remote_copy(
            src_ref=parts_ref.at[target],
            dst_ref=landed.at[offset],
            send_sem=send_sem.at[offset],
            recv_sem=recv_sem.at[offset],
            device_id=(target, 0, row),
            device_id_type=MESH,
        )
        copy.start()
        copies.append(copy)
    running = parts_ref[me].astype(jnp.float32)
    for offset in range(1, members):
        copies[offset - 1].wait_recv()
        running = running + landed[offset].astype(jnp.float32)
    total[...] = running
    swap = pltpu.make_async_remote_copy(
        src_ref=total,
        dst_ref=other,
        send_sem=row_send,
        recv_sem=row_recv,
        device_id=(me, 0, 1 - row),
        device_id_type=MESH,
    )
    swap.start()
    for copy in copies:
        copy.wait_send()
    swap.wait()
    out_ref[...] = total[...] + other[...]


def reduce_shares(parts):
    members = parts.shape[0]
    share = parts.shape[1:]
    dma = pltpu.SemaphoreType.DMA
    return pl.pallas_call(
        reduce_kernel,
        out_shape=jax.ShapeDtypeStruct(share, jnp.float32),
        in_specs=[pl.BlockSpec(memory_space=pltpu.VMEM)],
        out_specs=pl.BlockSpec(memory_space=pltpu.VMEM),
        scratch_shapes=[
            pltpu.VMEM(parts.shape, parts.dtype),
            pltpu.VMEM(share, jnp.float32),
            pltpu.VMEM(share, jnp.float32),
            dma((members,)),
            dma((members,)),
            dma,
            dma,
        ],
        compiler_params=pltpu.CompilerParams(collective_id=1, has_side_effects=True),
        name="reduce_shares",
    )(parts)


def direct_fits(projection_weight, output_weight, row_count):
    return (
        lax.axis_size("grp") == 2 * CHIPS
        and lax.axis_size("seq") == 1
        and lax.axis_size("prm") == 2
        and row_count == 128
        and projection_weight.shape[1] + output_weight.shape[1] // 2 == 3 * PART
        and projection_weight.shape[0] == 2 * output_weight.shape[0]
    )


def mm(a, b, contract=(1, 0)):
    return lax.dot_general(
        a, b, (((contract[0],), (contract[1],)), ((), ())), preferred_element_type=jnp.float32
    )


def block_kernel(
    step_ref,
    coef_ref,
    full_ref,
    before_ref,
    after_ref,
    means_ref,
    modulation_ref,
    query_gain_ref,
    key_gain_ref,
    down_ref,
    up_ref,
    out_down_ref,
    out_up_ref,
    parts_ref,
    qkv,
    out,
    inputs,
    projected,
    keep,
    att,
    grad_att,
    grad_proj,
    grad_vel,
    qkv_sem,
    out_sem,
):
    members = full_ref.shape[0]
    steps = step_ref.shape[0]
    rows = before_ref.shape[0]
    tokens = rows // steps
    head = query_gain_ref.shape[0]
    inner = out_down_ref.shape[0]
    heads = inner // head
    own_qkv = qkv.shape[0] // members
    half = out.shape[0] // members // 2
    scale = head ** (-0.5)

    copies, out_copies = [], []
    for g in range(members):
        copies.append(
            pltpu.make_async_copy(
                full_ref.at[g, pl.ds(0, own_qkv)],
                qkv.at[pl.ds(g * own_qkv, own_qkv)],
                qkv_sem.at[g],
            )
        )
    for g in range(members):
        for j in range(2):
            out_copies.append(
                pltpu.make_async_copy(
                    full_ref.at[g, pl.ds(own_qkv, half), pl.ds(j * inner, inner)],
                    out.at[pl.ds((2 * g + j) * half, half)],
                    out_sem.at[2 * g + j],
                )
            )
    for copy in copies + out_copies:
        copy.start()

    for s in range(steps):
        span = slice(s * tokens, (s + 1) * tokens)
        state = before_ref[span].astype(jnp.float32)
        centred = state - jnp.mean(state, axis=1, keepdims=True)
        spread = jnp.mean(centred * centred, axis=1, keepdims=True)
        rows_mod = modulation_ref[step_ref[s]]
        normed = centred * lax.rsqrt(spread + 1e-06)
        inputs[span] = (normed * (1.0 + rows_mod[1:2]) + rows_mod[0:1]).astype(jnp.bfloat16)
    low = mm(inputs[...], down_ref[...])
    low_t = low.T.astype(jnp.bfloat16)
    low_term = ADAPTER_SCALE * mm(up_ref[...], low_t, (0, 0))
    for g in range(members):
        span = slice(g * own_qkv, (g + 1) * own_qkv)
        copies[g].wait()
        projected[span] = mm(qkv[span], inputs[...], (1, 1)) + low_term[span]

    same = (lax.broadcasted_iota(jnp.int32, (rows, rows), 0) // tokens) == (
        lax.broadcasted_iota(jnp.int32, (rows, rows), 1) // tokens
    )

    def raw(which, h):
        start = which * inner + h * head
        return projected[start : start + head]

    def inverse_of(u):
        return lax.rsqrt(jnp.mean(u * u, axis=0, keepdims=True) + 1e-06)

    query_gain, key_gain = query_gain_ref[...], key_gain_ref[...]

    def query_of(h):
        u = raw(0, h)
        inverse = inverse_of(u)
        return u, inverse, (u * inverse * query_gain).astype(jnp.bfloat16)

    def key_of(h):
        u = raw(1, h)
        inverse = inverse_of(u)
        return u, inverse, (u * inverse * key_gain).astype(jnp.bfloat16)

    for h in range(heads):
        query, key = query_of(h)[2], key_of(h)[2]
        value = raw(2, h).astype(jnp.bfloat16)
        weights = jnp.where(same, jnp.exp(mm(key, query, (0, 0)) * scale), 0.0)
        probs = weights / jnp.sum(weights, axis=0, keepdims=True)
        keep[h] = probs
        att[h * head : (h + 1) * head] = mm(value, probs.astype(jnp.bfloat16)).astype(jnp.bfloat16)

    low_out = mm(att[...], out_down_ref[...], (0, 0)).astype(jnp.bfloat16)
    low_vel = ADAPTER_SCALE * mm(low_out, out_up_ref[...])
    for copy in out_copies:
        copy.wait()
    velocity = mm(out[...], att[...]).T + low_vel
    step_size = 1.0 / SCHED
    for s in range(steps):
        span = slice(s * tokens, (s + 1) * tokens)
        coupling, rest, inverse, advantage, factor = (coef_ref[s, i] for i in range(5))
        state = before_ref[span].astype(jnp.float32)
        vel = velocity[span]
        mean_now = state - step_size * (vel + coupling * (state + rest * vel))
        residual = after_ref[span].astype(jnp.float32) - mean_now
        drift = mean_now - means_ref[span].astype(jnp.float32)
        grad_mean = (BETA * drift - advantage * residual) * inverse
        grad_vel[span] = (grad_mean * factor).astype(jnp.bfloat16)
    gv = grad_vel[...]
    out_up_grad = ADAPTER_SCALE * mm(low_out, gv, (0, 0))
    grad_low = ADAPTER_SCALE * mm(gv, out_up_ref[...], (1, 1))
    grad_low_t = grad_low.T.astype(jnp.bfloat16)
    out_down_grad = mm(grad_low_t, att[...], (1, 1))
    grad_att_rows = mm(gv, out[...]) + mm(
        grad_low.astype(jnp.bfloat16), out_down_ref[...], (1, 1)
    )
    grad_att[...] = grad_att_rows.T.astype(jnp.bfloat16)

    def back(u, inverse, gain, e):
        scaled = e * gain
        return inverse * scaled - u * (inverse * inverse * inverse) * jnp.mean(
            scaled * u, axis=0, keepdims=True
        )

    for h in range(heads):
        span = slice(h * head, (h + 1) * head)
        query_raw, query_inverse, query = query_of(h)
        key_raw, key_inverse, key = key_of(h)
        value = raw(2, h).astype(jnp.bfloat16)
        probs = keep[h]
        upstream = grad_att[span]
        grad_probs = mm(value, upstream, (0, 0))
        delta = jnp.sum(
            upstream.astype(jnp.float32) * att[span].astype(jnp.float32), axis=0, keepdims=True
        )
        grad_scores = (probs * (grad_probs - delta) * scale).astype(jnp.bfloat16)
        grad_query = mm(key, grad_scores)
        grad_key = mm(query, grad_scores, (1, 1)).astype(jnp.bfloat16).astype(jnp.float32)
        grad_value = mm(upstream, probs.astype(jnp.bfloat16), (1, 1)).astype(jnp.bfloat16)
        first, second, third = (i * inner + h * head for i in range(3))
        grad_proj[first : first + head] = back(
            query_raw, query_inverse, query_gain, grad_query
        ).astype(jnp.bfloat16)
        grad_proj[second : second + head] = back(
            key_raw, key_inverse, key_gain, grad_key
        ).astype(jnp.bfloat16)
        grad_proj[third : third + head] = grad_value

    up_grad = ADAPTER_SCALE * mm(low_t, grad_proj[...], (1, 1))
    grad_low_qkv = (ADAPTER_SCALE * mm(up_ref[...], grad_proj[...])).astype(jnp.bfloat16)
    down_grad = mm(grad_low_qkv, inputs[...])
    at = 0
    for grad in (down_grad, up_grad, out_down_grad, out_up_grad):
        width = grad.shape[1] // members
        for g in range(members):
            parts_ref[g, :, at : at + width] = grad[:, g * width : (g + 1) * width].astype(
                jnp.bfloat16
            )
        at += width


def block_gradients(steps, coef, full, *rest):
    before, query_gain, out_down, out_up = rest[0], rest[4], rest[8], rest[9]
    up = rest[7]
    members = full.shape[0]
    rows, width = before.shape
    inner, rank = out_down.shape
    heads = inner // query_gain.shape[0]
    share = (2 * width + 4 * inner) // members
    bf, f32, dma = jnp.bfloat16, jnp.float32, pltpu.SemaphoreType.DMA
    vmem = pl.BlockSpec(memory_space=pltpu.VMEM)
    smem = pl.BlockSpec(memory_space=pltpu.SMEM)
    return pl.pallas_call(
        block_kernel,
        out_shape=jax.ShapeDtypeStruct((members, rank, share), bf),
        in_specs=[smem, smem, pl.BlockSpec(memory_space=pl.ANY)] + [vmem] * len(rest),
        out_specs=vmem,
        scratch_shapes=[
            pltpu.VMEM((3 * inner, width), bf),
            pltpu.VMEM((width, inner), bf),
            pltpu.VMEM((rows, width), bf),
            pltpu.VMEM((3 * inner, rows), f32),
            pltpu.VMEM((heads, rows, rows), f32),
            pltpu.VMEM((inner, rows), bf),
            pltpu.VMEM((inner, rows), bf),
            pltpu.VMEM((3 * inner, rows), bf),
            pltpu.VMEM((rows, width), bf),
            dma((members,)),
            dma((2 * members,)),
        ],
        compiler_params=pltpu.CompilerParams(vmem_limit_bytes=48 * 1024 * 1024),
        name="block_gradients",
    )(steps, coef, full, *rest)


def split_share(share, widths):
    first, second, third = widths[0], widths[0] + widths[1], sum(widths[:3])
    return (
        share[:, :first].T,
        share[:, first:second],
        share[:, second:third].T,
        share[:, third:],
    )


def per_device(
    latent_before_step,
    latent_after_step,
    reference_step_means,
    rewards,
    sample_prompt_index,
    stored_step_index,
    modulation,
    projection_weight,
    output_weight,
    query_norm_gain,
    key_norm_gain,
    projection_down_weight,
    projection_up_weight,
    output_down_weight,
    output_up_weight,
):
    steps_here = latent_before_step.shape[2]
    local_tokens = latent_before_step.shape[3]
    model_width = latent_before_step.shape[4]
    head_size = query_norm_gain.shape[0]
    inner_width = output_weight.shape[0]
    head_count = inner_width // head_size
    grp_count = lax.axis_size("grp")
    row_count = steps_here * local_tokens
    score_scale = head_size ** (-0.5)
    step_size = 1.0 / SCHED
    sample_number = lax.axis_size("prm") * grp_count * steps_here
    member = (sample_prompt_index[0, 0] == jnp.arange(2, dtype=jnp.int32)).astype(jnp.float32)
    reward = rewards[0, 0]
    direct = direct_fits(projection_weight, output_weight, row_count)
    if direct:
        half = output_weight.shape[1] // 2
        qkv_own = projection_weight.shape[1]
        own_out = output_weight.T
        own = jnp.concatenate(
            [projection_weight.T, jnp.concatenate([own_out[:half], own_out[half:]], axis=1)],
            axis=0,
        )
        note = jnp.broadcast_to(
            jnp.pad(member * reward, (0, 6))[:, None], (8, 128)
        )
        full, notes = gather_weights(own, note)
        totals = jnp.sum(notes[:, :2, 0], axis=0)
        advantage = reward - jnp.sum(member * totals) / (grp_count // 2)
        timestep_values = stored_step_index[0, 0]
        time_now = 1.0 - timestep_values.astype(jnp.float32) / SCHED
        variance = ETA * ETA * time_now / (1.0 - time_now) / SCHED
        coupling = ETA * ETA / (2.0 * (1.0 - time_now))
        coef = jnp.stack(
            [
                coupling,
                1.0 - time_now,
                1.0 / (sample_number * variance),
                jnp.broadcast_to(advantage, coupling.shape),
                -step_size * (1.0 + coupling * (1.0 - time_now)),
            ],
            axis=1,
        )
        parts = block_gradients(
            timestep_values,
            coef,
            full,
            latent_before_step.reshape(row_count, model_width),
            latent_after_step.reshape(row_count, model_width),
            reference_step_means.reshape(row_count, model_width),
            modulation,
            query_norm_gain[:, None],
            key_norm_gain[:, None],
            projection_down_weight,
            projection_up_weight,
            output_down_weight,
            output_up_weight,
        )
        widths = [size // grp_count for size in (model_width, 3 * inner_width, inner_width)]
        return split_share(reduce_shares(parts), widths)
    totals = lax.psum(member * reward, "grp")
    full_qkv, full_out = (
        lax.all_gather(projection_weight.T, "grp", axis=0, tiled=True),
        lax.all_gather(output_weight.T, "grp", axis=0, tiled=True),
    )
    advantage_values = reward - jnp.sum(member * totals) / (grp_count // 2)
    timestep_values = stored_step_index[0, 0]
    time_now = 1.0 - timestep_values.astype(jnp.float32) / SCHED
    variance = ETA * ETA * time_now / (1.0 - time_now) / SCHED
    coupling = ETA * ETA / (2.0 * (1.0 - time_now))
    mod_rows = jnp.take(modulation, timestep_values, axis=0)
    shift_rows = mod_rows[:, 0][:, None, :]
    scale_rows = mod_rows[:, 1][:, None, :]
    state_now = latent_before_step[0, 0].astype(jnp.float32)
    centre = jnp.mean(state_now, axis=-1, keepdims=True)
    spread = jnp.mean((state_now - centre) ** 2, axis=-1, keepdims=True)
    normed = (state_now - centre) * lax.rsqrt(spread + 1e-06)
    input_rows = (
        (normed * (1.0 + scale_rows) + shift_rows)
        .astype(jnp.bfloat16)
        .reshape(row_count, model_width)
    )
    projection_lowrank = jnp.dot(
        input_rows, projection_down_weight, preferred_element_type=jnp.float32
    ).astype(jnp.bfloat16)
    projected_rows = jnp.einsum(
        "rk,ck->rc", input_rows, full_qkv, preferred_element_type=jnp.float32
    ) + ADAPTER_SCALE * jnp.dot(
        projection_lowrank, projection_up_weight, preferred_element_type=jnp.float32
    )
    projected_rows = projected_rows.reshape(steps_here, local_tokens, 3, head_count, head_size)
    query_raw = projected_rows[:, :, 0]
    key_raw = projected_rows[:, :, 1]
    value_raw = projected_rows[:, :, 2]
    query_norm, query_inverse = rms_forward(query_raw, query_norm_gain)
    key_norm, key_inverse = rms_forward(key_raw, key_norm_gain)
    query_heads = jnp.transpose(query_norm.astype(jnp.bfloat16), (0, 2, 1, 3))
    key_local = jnp.transpose(key_norm.astype(jnp.bfloat16), (0, 2, 3, 1))
    value_local = jnp.transpose(value_raw.astype(jnp.bfloat16), (0, 2, 3, 1))
    key_cols, value_cols = (
        lax.all_gather(key_local, "seq", axis=3, tiled=True),
        lax.all_gather(value_local, "seq", axis=3, tiled=True),
    )
    scores = (
        jnp.einsum("shqd,shdk->shqk", query_heads, key_cols, preferred_element_type=jnp.float32)
        * score_scale
    )
    weights = jnp.exp(scores)
    attn_probs = weights / jnp.sum(weights, axis=-1, keepdims=True)
    probs_bf = attn_probs.astype(jnp.bfloat16)
    attended_heads = jnp.einsum(
        "shqk,shdk->shqd", probs_bf, value_cols, preferred_element_type=jnp.float32
    ).astype(jnp.bfloat16)
    attended_token_rows = jnp.transpose(attended_heads, (0, 2, 1, 3)).reshape(
        row_count, inner_width
    )
    output_lowrank = jnp.dot(
        attended_token_rows, output_down_weight, preferred_element_type=jnp.float32
    ).astype(jnp.bfloat16)
    predicted_velocity = jnp.einsum(
        "rk,ck->rc", attended_token_rows, full_out, preferred_element_type=jnp.float32
    ) + ADAPTER_SCALE * jnp.dot(
        output_lowrank, output_up_weight, preferred_element_type=jnp.float32
    )
    predicted_velocity = predicted_velocity.reshape(steps_here, local_tokens, model_width)
    time_col = time_now[:, None, None]
    var_col = variance[:, None, None]
    coup_col = coupling[:, None, None]
    mean_now = state_now - step_size * (
        predicted_velocity + coup_col * (state_now + (1.0 - time_col) * predicted_velocity)
    )
    residual = latent_after_step[0, 0].astype(jnp.float32) - mean_now
    ref_drift = mean_now - reference_step_means[0, 0].astype(jnp.float32)
    grad_mean = (-advantage_values * residual + BETA * ref_drift) / (sample_number * var_col)
    velocity_gradient = (
        (grad_mean * (-step_size * (1.0 + coup_col * (1.0 - time_col))))
        .astype(jnp.bfloat16)
        .reshape(row_count, model_width)
    )
    output_up_gradient = ADAPTER_SCALE * jnp.dot(
        output_lowrank.T, velocity_gradient, preferred_element_type=jnp.float32
    )
    output_lowrank_gradient = (
        ADAPTER_SCALE
        * jnp.dot(velocity_gradient, output_up_weight.T, preferred_element_type=jnp.float32)
    ).astype(jnp.bfloat16)
    grad_a_out = jnp.dot(
        attended_token_rows.T, output_lowrank_gradient, preferred_element_type=jnp.float32
    )
    attended_gradient = jnp.dot(
        velocity_gradient, full_out, preferred_element_type=jnp.float32
    ) + jnp.dot(output_lowrank_gradient, output_down_weight.T, preferred_element_type=jnp.float32)
    grad_att_heads = jnp.transpose(
        attended_gradient.astype(jnp.bfloat16).reshape(
            steps_here, local_tokens, head_count, head_size
        ),
        (0, 2, 1, 3),
    )
    grad_probs = jnp.einsum(
        "shqd,shdk->shqk", grad_att_heads, value_cols, preferred_element_type=jnp.float32
    )
    row_delta = jnp.sum(
        grad_att_heads.astype(jnp.float32) * attended_heads.astype(jnp.float32),
        axis=-1,
        keepdims=True,
    )
    grad_scores = (attn_probs * (grad_probs - row_delta) * score_scale).astype(jnp.bfloat16)
    grad_query_heads = jnp.einsum(
        "shqk,shdk->shqd", grad_scores, key_cols, preferred_element_type=jnp.float32
    )
    grad_query = jnp.transpose(grad_query_heads, (0, 2, 1, 3))
    key_term = jnp.einsum(
        "shqk,shqd->shdk", grad_scores, query_heads, preferred_element_type=jnp.float32
    )
    value_term = jnp.einsum(
        "shqk,shqd->shdk", probs_bf, grad_att_heads, preferred_element_type=jnp.float32
    )
    key_owned, value_owned = (
        lax.psum_scatter(
            key_term.astype(jnp.bfloat16), "seq", scatter_dimension=3, tiled=True
        ).astype(jnp.float32),
        lax.psum_scatter(
            value_term.astype(jnp.bfloat16), "seq", scatter_dimension=3, tiled=True
        ).astype(jnp.float32),
    )
    grad_key = jnp.transpose(key_owned, (0, 3, 1, 2))
    grad_value = jnp.transpose(value_owned, (0, 3, 1, 2))
    grad_q_raw = rms_backward(query_raw, query_inverse, query_norm_gain, grad_query)
    grad_k_raw = rms_backward(key_raw, key_inverse, key_norm_gain, grad_key)
    projected_gradient = (
        jnp.stack([grad_q_raw, grad_k_raw, grad_value], axis=2)
        .astype(jnp.bfloat16)
        .reshape(row_count, 3 * inner_width)
    )
    projection_up_gradient = ADAPTER_SCALE * jnp.dot(
        projection_lowrank.T, projected_gradient, preferred_element_type=jnp.float32
    )
    projection_lowrank_gradient = (
        ADAPTER_SCALE
        * jnp.dot(projected_gradient, projection_up_weight.T, preferred_element_type=jnp.float32)
    ).astype(jnp.bfloat16)
    grad_a_qkv = jnp.dot(
        input_rows.T, projection_lowrank_gradient, preferred_element_type=jnp.float32
    )
    local_grads = (grad_a_qkv, projection_up_gradient, grad_a_out, output_up_gradient)
    rank = projection_lowrank.shape[1]
    wide = (local_grads[0].T, local_grads[1], local_grads[2].T, local_grads[3])
    widths = [grad.shape[1] // grp_count for grad in wide]
    packed = jnp.concatenate(
        [
            grad.astype(jnp.bfloat16).reshape(rank, grp_count, width)
            for grad, width in zip(wide, widths)
        ],
        axis=2,
    )
    share = lax.psum_scatter(packed, "grp", scatter_dimension=1, tiled=True)
    share = lax.psum(share.astype(jnp.float32).reshape(rank, -1), ("seq", "prm"))
    return split_share(share, widths)


def solution(mesh):
    in_specs = (
        P("prm", "grp", None, "seq", None),
        P("prm", "grp", None, "seq", None),
        P("prm", "grp", None, "seq", None),
        P("prm", "grp"),
        P("prm", "grp"),
        P("prm", "grp", None),
        P(),
        P(None, "grp"),
        P(None, "grp"),
        P(),
        P(),
        P(),
        P(),
        P(),
        P(),
    )
    out_specs = (P("grp", None), P(None, "grp"), P("grp", None), P(None, "grp"))
    return jax.shard_map(
        per_device, mesh=mesh, in_specs=in_specs, out_specs=out_specs, check_vma=False
    )
```
